32 devices in a mesh: dp: 16 (over z, y, x), mp: 2 (over core).
Axes of the slice: x: 2, y: 2, z: 4, core: 2. Of those that a mesh axis runs over, the one named last changes fastest.
Arguments:
- hist: bfloat16 [13, 2048, 2048], P(None, 'dp', 'mp'), may hold values from -6 to 6
- mixin: float32 [2048, 52], P('dp'), may hold values from -1.8 to 1.8
- seg_ids: int32 [32, 64], P('dp'), may hold values from 0 to 3, never falling along the last dimension, each value on 1 to 32 neighbouring positions
- domain_ids: int32 [2048], P('dp'), may hold values from 0 to 7
- loss_table: float32 [8], replicated, may hold values from 0.25 to 2
- w_qkv: bfloat16 [3, 2048, 2048], P(None, 'dp', 'mp'), may hold values from -0.125 to 0.125
- w_o: bfloat16 [2048, 2048], P('mp', 'dp'), may hold values from -0.5 to 0.5
- w_up: bfloat16 [2048, 8192], P('dp', 'mp'), may hold values from -0.125 to 0.125
- w_down: bfloat16 [8192, 2048], P('mp', 'dp'), may hold values from -0.0625 to 0.0625
- mix_w1: bfloat16 [2048, 56], P('dp'), may hold values from -0.125 to 0.125
- mix_w2: bfloat16 [56, 56], replicated, may hold values from -0.75 to 0.75
- norm_gain: bfloat16 [5, 2048], P(None, 'dp'), may hold values from 0.5 to 1.5
- norm_bias: bfloat16 [4, 2048], P(None, 'dp'), may hold values from -1.1953125 to 1.1953125
- out_cot: bfloat16 [2048, 2048], P('dp'), may hold values from -6 to 6
- mix_cot: float32 [2048, 56], P('dp'), may hold values from -6 to 6
Outputs:
- block_out: bfloat16 [2048, 2048], P('dp')
- mix_out: float32 [2048, 56], P('dp')
- hist_grad: float32 [13, 2048, 2048], P(None, 'dp', 'mp')
- mixin_grad: float32 [2048, 52], P('dp')
- w_qkv_grad: float32 [3, 2048, 2048], P(None, 'dp', 'mp')
- w_o_grad: float32 [2048, 2048], P('mp', 'dp')
- w_up_grad: float32 [2048, 8192], P('dp', 'mp')
- w_down_grad: float32 [8192, 2048], P('mp', 'dp')
- mix_w1_grad: float32 [2048, 56], P('dp')
- mix_w2_grad: float32 [56, 56], replicated
- gain_grad: float32 [5, 2048], P(None, 'dp')
- bias_grad: float32 [4, 2048], P(None, 'dp')
The draws below stay inside these ranges and needn't reach their ends.
Inputs may be any that keep to these rules, and one draw needn't show every extreme that they name: `seg_ids`: along each sequence the numbers never fall; a document has at most 32 tokens, and some has exactly that many.
All inputs are finite; a program needn't handle non-finite values.
Results may differ from the reference program's by a relative error of at most 0.015.
Values may be sent and summed in bfloat16 or wider, within the bound.
No kernel may reach another device: no remote copies, remote signals or barrier semaphores. Data moves between devices by JAX's collectives and lax.ppermute only.
A program may use at most 256 MiB of HBM per device.

```python
import math
import jax
import jax.numpy as jnp
import numpy as np
from jax import lax

D = 2048
HEADS = 16
HDIM = 128
FF = 8192
ROT = 32
HIST = 13
MIXH = 56
MIXO = 56
GROUPS = 8
SEQ = 64
SEQS = 32
TOKENS = 2048


def touch_ends(array, rng, least, high):
    longest = array.shape.index(max(array.shape))
    spots = []
    for shift in (0, 1):
        where = [jax.random.randint(jax.random.fold_in(rng, axis), (), 0, length) for axis, length in enumerate(array.shape)]
        where[longest] = (where[longest] + shift) % array.shape[longest]
        spots.append(tuple(where))
    return array.at[spots[0]].set(least).at[spots[1]].set(high)


def block_levels(stream_key, dims, split, least, top_value):
    level, own = 1.0, jax.random.fold_in(stream_key, 6)
    for axis_at, shards_of in split:
        steps = jnp.exp(jax.random.uniform(jax.random.fold_in(own, axis_at), (shards_of,), jnp.float32, least / len(split), top_value / len(split)))
        level = level * jnp.repeat(steps, dims[axis_at] // shards_of).reshape([-1 if axis == axis_at else 1 for axis in range(len(dims))])
    return level


def cumulative_ranks(number_of, skew):
    weights = [(1 << 20) // math.isqrt(rank ** skew) + 1 for rank in range(1, number_of + 1)]
    deviation = 1 + sum(weights) // (1 << 30)
    return np.cumsum(np.array([max(1, weight // deviation) for weight in weights]))


def ranked(key, shape, amount, lean):
    grid = cumulative_ranks(amount, lean)
    pick = jax.random.randint(jax.random.fold_in(key, 1), shape, 0, int(grid[amount - 1]))
    grade = jnp.searchsorted(jnp.asarray(grid, jnp.int32), pick, side="right")
    return jax.random.permutation(jax.random.fold_in(key, 2), amount)[grade].astype(jnp.int32)


def split_up(count, total, most, lean):
    loads = [(1 << 20) // math.isqrt(standing ** lean) + 1 for standing in range(2, count + 1)]
    surplus, holding = total - most - (count - 1), [1] * (count - 1)
    while surplus > 0:
        free = [i for i in range(count - 1) if holding[i] < most]
        whole, left = sum([loads[i] for i in free]), surplus
        for i in free:
            addition = min(most - holding[i], max(1, left * loads[i] // whole), surplus)
            holding[i] = holding[i] + addition
            surplus = surplus - addition
    return np.array([most] + holding)


def ragged_sizes(rng, amount, total, reach, slope):
    if amount == 2:
        one = jax.random.randint(rng, (), max(1, total - reach), min(reach, total - 1) + 1)
        return jnp.stack([one, total - one])
    tallies = jnp.asarray(split_up(amount, total, reach, slope), jnp.int32)
    twos = (amount - 1) // 2
    donor, receiver = tallies[1:1 + 2 * twos:2], tallies[2:2 + 2 * twos:2]
    room = jnp.minimum(donor - 1, reach - receiver)
    shifted = jax.random.randint(jax.random.fold_in(rng, 1), (twos,), 0, 1 << 20) % (room + 1)
    tallies = tallies.at[1:1 + 2 * twos:2].set(donor - shifted).at[2:2 + 2 * twos:2].set(receiver + shifted)
    return tallies[jax.random.permutation(jax.random.fold_in(rng, 2), amount)]


def noise(rng, shape, scale, limit, cuts=(), held_as=jnp.bfloat16):
    values = scale * jax.random.normal(rng, shape, jnp.float32)
    if cuts:
        values = values * block_levels(rng, shape, cuts, -0.22, 0.18)
    return jnp.clip(values, -limit, limit).astype(held_as)


def setup_inputs(seed: int = 0) -> dict:
    arg_keys = jax.random.split(jax.random.key(seed), 16)
    return {
        "hist": noise(arg_keys[0], (HIST, TOKENS, D), 1.0, 6.0, ((1, 16), (2, 2))),
        "mixin": noise(arg_keys[1], (TOKENS, 4 * HIST), 0.3, 1.8, ((0, 16),), jnp.float32),
        "seg_ids": jax.vmap(lambda own: jnp.searchsorted(jnp.cumsum(ragged_sizes(own, 4, SEQ, SEQ // 2, 2)), jnp.arange(SEQ), side="right"))(jax.random.split(arg_keys[2], SEQS)).reshape((SEQS, SEQ)).astype(jnp.int32),
        "domain_ids": touch_ends(ranked(arg_keys[3], (TOKENS,), GROUPS, 2), jax.random.fold_in(arg_keys[3], 3), 0, GROUPS - 1).astype(jnp.int32),
        "loss_table": jnp.clip(jnp.exp(jax.random.uniform(arg_keys[4], (GROUPS,), jnp.float32, math.log(0.25), math.log(2.0))), 0.25, 2.0),
        "w_qkv": noise(arg_keys[5], (3, D, D), D ** -0.5, 0.125, ((1, 16), (2, 2))),
        "w_o": noise(arg_keys[6], (D, D), (D // 16) ** -0.5, 0.5, ((0, 2), (1, 16))),
        "w_up": noise(arg_keys[7], (D, FF), D ** -0.5, 0.125, ((0, 16), (1, 2))),
        "w_down": noise(arg_keys[8], (FF, D), FF ** -0.5, 0.0625, ((0, 2), (1, 16))),
        "mix_w1": noise(arg_keys[9], (D, MIXH), D ** -0.5, 0.125, ((0, 16),)),
        "mix_w2": noise(arg_keys[10], (MIXH, MIXO), MIXH ** -0.5, 0.75),
        "norm_gain": jnp.clip(1.0 + 0.1 * jax.random.normal(arg_keys[11], (5, D), jnp.float32), 0.5, 1.5).astype(jnp.bfloat16),
        "norm_bias": noise(arg_keys[12], (4, D), 0.2, 1.1953125, ((1, 16),)),
        "out_cot": noise(arg_keys[13], (TOKENS, D), 1.0, 6.0, ((0, 16),)),
        "mix_cot": noise(arg_keys[14], (TOKENS, MIXO), 1.0, 6.0, ((0, 16),), jnp.float32),
    }


@jax.custom_vjp
def low(v):
    return lax.optimization_barrier(v.astype(jnp.bfloat16)).astype(jnp.float32)

@jax.custom_vjp
def low_back(v):
    return v

def low_keep(v):
    return (low(v), None)

def low_pass(kept, grad):
    return (grad,)

def back_keep(v):
    return (v, None)

def back_low(kept, grad):
    return (low(grad),)
low.defvjp(low_keep, low_pass)
low_back.defvjp(back_keep, back_low)
highest = lax.Precision.HIGHEST
eps_norm = 1e-05
eps_rms = 1e-06

def layer_norm(values, gain_row, bias_row):
    center = values - lax.optimization_barrier(jnp.mean(values, axis=-1, keepdims=True))
    spread = lax.optimization_barrier(jnp.mean(center * center, axis=-1, keepdims=True))
    return center * lax.rsqrt(spread + eps_norm) * gain_row + bias_row

def rms_scale(values, gain_row):
    return values * lax.rsqrt(lax.optimization_barrier(jnp.mean(values * values, axis=-1, keepdims=True)) + eps_rms) * gain_row

def exact_gelu(values):
    return jax.nn.gelu(values, approximate=False)

def rotary_tables(length, rotated):
    half_rot = rotated // 2
    frequency = 10000.0 ** (-2.0 * jnp.arange(half_rot, dtype=jnp.float32) / rotated)
    angles = jnp.arange(length, dtype=jnp.float32)[:, None] * frequency[None, :]
    return (jnp.cos(angles), jnp.sin(angles))

def rotate(values, cosine_table, sine_table, rotated):
    half_rot = rotated // 2
    first_part = values[..., :half_rot]
    second = values[..., half_rot:rotated]
    cosine_b = cosine_table[:, None, :]
    sine_b = sine_table[:, None, :]
    return jnp.concatenate([first_part * cosine_b - second * sine_b, second * cosine_b + first_part * sine_b, values[..., rotated:]], axis=-1)

def attend_one(pieces):
    queries, keys_in, values_in, segment = pieces
    scores = jnp.einsum('qhd,khd->hqk', queries, keys_in, precision=highest) * HDIM ** (-0.5)
    scores = low_back(scores)
    positions = jnp.arange(SEQ)
    allowed = (positions[:, None] >= positions[None, :]) & (segment[:, None] == segment[None, :])
    scores = jnp.where(allowed[None], scores, -1e+30)
    weights = low(jax.nn.softmax(scores, axis=-1))
    return jnp.einsum('hqk,khd->qhd', weights, values_in, precision=highest)

def forward(hist, mixin, w_qkv, w_o, w_up, w_down, mix_w1, mix_w2, norm_gain, norm_bias, seg_ids):
    tokens = hist.shape[1]
    blend = mixin.reshape(tokens, 4, HIST)
    streams = jnp.einsum('tsj,jtd->std', blend, hist, precision=highest)
    normed = [low(layer_norm(streams[stream_id], norm_gain[stream_id], norm_bias[stream_id])) for stream_id in range(3)]
    cosine_table, sine_table = rotary_tables(SEQ, ROT)

    def heads_of(values):
        return values.reshape(tokens // SEQ, SEQ, HEADS, HDIM)
    query_pre = low_back(jnp.dot(normed[0], w_qkv[0], precision=highest, preferred_element_type=jnp.float32))
    key_pre = low_back(jnp.dot(normed[1], w_qkv[1], precision=highest, preferred_element_type=jnp.float32))
    value_pre = low_back(jnp.dot(normed[2], w_qkv[2], precision=highest, preferred_element_type=jnp.float32))
    queries = low(rotate(heads_of(query_pre), cosine_table, sine_table, ROT))
    keys_in = low(rotate(heads_of(key_pre), cosine_table, sine_table, ROT))
    values_in = low(heads_of(value_pre))
    attended = lax.map(jax.checkpoint(attend_one), (queries, keys_in, values_in, seg_ids))
    context = low(low_back(attended.reshape(tokens, D)))
    attention = low_back(jnp.dot(context, w_o, precision=highest, preferred_element_type=jnp.float32))
    resid = streams[3] + attention
    ffn_in = low(layer_norm(resid, norm_gain[3], norm_bias[3]))
    up_pre = low_back(jnp.dot(ffn_in, w_up, precision=highest, preferred_element_type=jnp.float32))
    active = low(exact_gelu(up_pre))
    ffn_out = low_back(jnp.dot(active, w_down, precision=highest, preferred_element_type=jnp.float32))
    block_value = resid + ffn_out
    mix_in = low(rms_scale(block_value, norm_gain[4]))
    mix_pre = jnp.dot(mix_in, mix_w1, precision=highest, preferred_element_type=jnp.float32)
    mix_act = low(exact_gelu(mix_pre))
    mix_out = jnp.dot(mix_act, mix_w2, precision=highest, preferred_element_type=jnp.float32)
    return (block_value, mix_out)

def reference(hist, mixin, seg_ids, domain_ids, loss_table, w_qkv, w_o, w_up, w_down, mix_w1, mix_w2, norm_gain, norm_bias, out_cot, mix_cot):
    floats = [arg_value.astype(jnp.float32) for arg_value in (hist, mixin, w_qkv, w_o, w_up, w_down, mix_w1, mix_w2, norm_gain, norm_bias)]

    def run_forward(*values):
        return forward(*values, seg_ids)
    (block_value, mix_out), pull = jax.vjp(run_forward, *floats)
    token_weight = loss_table.astype(jnp.float32)[domain_ids][:, None]
    gradients = pull((out_cot.astype(jnp.float32) * token_weight, mix_cot.astype(jnp.float32) * token_weight))
    return (block_value.astype(jnp.bfloat16), mix_out, gradients[0], gradients[1], gradients[2], gradients[3], gradients[4], gradients[5], gradients[6], gradients[7], gradients[8], gradients[9])
```

```python
import jax
import jax.numpy as jnp
from jax import lax
from jax.sharding import Mesh
from jax.sharding import PartitionSpec as P

HDIM = 128
ROT = 32
INNER = 4


highest = lax.Precision.HIGHEST
eps_norm = 1e-05
eps_rms = 1e-06
low = jnp.bfloat16
wide = jnp.float32


def layer_norm(values, gain_row, bias_row):
    center = values - jnp.mean(values, axis=-1, keepdims=True)
    spread = jnp.mean(center * center, axis=-1, keepdims=True)
    return center * lax.rsqrt(spread + eps_norm) * gain_row + bias_row


def rms_scale(values, gain_row):
    return (
        values * lax.rsqrt(jnp.mean(values * values, axis=-1, keepdims=True) + eps_rms) * gain_row
    )


def exact_gelu(values):
    return jax.nn.gelu(values, approximate=False)


def rotary_tables(length, rotated):
    half_rot = rotated // 2
    frequency = 10000.0 ** (-2.0 * jnp.arange(half_rot, dtype=wide) / rotated)
    angles = jnp.arange(length, dtype=wide)[:, None] * frequency[None, :]
    return (jnp.cos(angles), jnp.sin(angles))


def rotate(values, cosine_table, sine_table):
    half_rot = ROT // 2
    first_part = values[..., :half_rot]
    second = values[..., half_rot:ROT]
    cosine_b = cosine_table[:, None, :]
    sine_b = sine_table[:, None, :]
    return jnp.concatenate(
        [
            first_part * cosine_b - second * sine_b,
            second * cosine_b + first_part * sine_b,
            values[..., ROT:],
        ],
        axis=-1,
    )


def dot(left, right):
    return jnp.dot(left, right, preferred_element_type=wide)


def outer_sum(left_rows, right_rows):
    return lax.dot_general(
        left_rows, right_rows, (((0,), (0,)), ((), ())), preferred_element_type=wide
    )


def across(grad_rows, weight):
    return lax.dot_general(
        grad_rows, weight, (((1,), (1,)), ((), ())), preferred_element_type=wide
    )


def swap(values):
    return lax.ppermute(values, "mp", [(0, 1), (1, 0)])


def hop(values, axis, distance):
    count = lax.axis_size(axis)
    return lax.ppermute(values, axis, [(spot, spot ^ distance) for spot in range(count)])


def spread_out(values, axis):
    return [values] + [hop(values, axis, k) for k in range(1, lax.axis_size(axis))]


def trade(pick, axis):
    return [pick(0)] + [hop(pick(k), axis, k) for k in range(1, lax.axis_size(axis))]


def in_order(blocks, axis):
    own = lax.axis_index(axis)
    stacked = jnp.zeros((len(blocks),) + blocks[0].shape, blocks[0].dtype)
    for k, block in enumerate(blocks):
        stacked = lax.dynamic_update_index_in_dim(stacked, block, own ^ k, 0)
    return stacked


def gather_tokens(rows, axis):
    own = jnp.concatenate(spread_out(rows, axis), axis=-2)
    return jnp.concatenate([own, swap(own)], axis=-2)


def reduce_tokens(partial_of, axis):
    count = lax.axis_size(axis)
    theirs = partial_of(1).astype(low)
    mine = partial_of(0)
    mine = mine + swap(theirs).astype(wide)
    blocks = jnp.split(mine, count, axis=-2)
    got = trade(lambda k: blocks[k] if k == 0 else blocks[k].astype(low), axis)
    total = got[0]
    for block in got[1:]:
        total = total + block.astype(wide)
    return total


def add_over(values, axis):
    distance = 1
    while distance < lax.axis_size(axis):
        values = values + hop(values, axis, distance)
        distance *= 2
    return values


def scatter_features(rows):
    count_a, count_b = lax.axis_size("a"), lax.axis_size("b")
    own_a, own_b = lax.axis_index("a"), lax.axis_index("b")
    height = rows.shape[0]
    rows = rows + swap(rows)
    by_a = rows.reshape(height, count_a, -1)
    got = trade(lambda k: lax.dynamic_index_in_dim(by_a, own_a ^ k, 1, keepdims=False), "a")
    rows = sum(got[1:], got[0])
    by_b = rows.reshape(height, count_b, -1)
    got = trade(lambda k: lax.dynamic_index_in_dim(by_b, own_b ^ k, 1, keepdims=False), "b")
    return sum(got[1:], got[0])


def gather_features(rows):
    height = rows.shape[0]
    rows = in_order(spread_out(rows, "b"), "b")
    rows = in_order(spread_out(rows, "a"), "a")
    return jnp.moveaxis(rows, 2, 0).reshape(height, -1)


def body(
    hist,
    mixin,
    seg_ids,
    domain_ids,
    loss_table,
    w_qkv,
    w_o,
    w_up,
    w_down,
    mix_w1,
    mix_w2,
    norm_gain,
    norm_bias,
    out_cot,
    mix_cot,
):
    count_a, count_b, count_c = lax.axis_size("a"), lax.axis_size("b"), lax.axis_size("mp")
    own_a, own_b, own_c = lax.axis_index("a"), lax.axis_index("b"), lax.axis_index("mp")
    depth_hist, chip_tokens, half_width = hist.shape
    length = seg_ids.shape[1]
    width = half_width * count_c
    score_scale = HDIM ** (-0.5)
    rows_here = chip_tokens // count_c
    first = own_c == 0

    def own_rows(values, axis=0):
        return lax.dynamic_slice_in_dim(values, own_c * rows_here, rows_here, axis)

    def other_rows(values, axis=0):
        return lax.dynamic_slice_in_dim(values, (1 - own_c) * rows_here, rows_here, axis)

    def both(mine, theirs, axis):
        return jnp.concatenate(
            [jnp.where(first, mine, theirs), jnp.where(first, theirs, mine)], axis=axis
        )

    group_qkv = w_qkv.shape[2] // count_b
    qkv_parts = trade(
        lambda k: lax.dynamic_slice_in_dim(w_qkv, (own_b ^ k) * group_qkv, group_qkv, 2), "b"
    )
    qkv_rows = jnp.moveaxis(in_order(qkv_parts, "b"), 0, 1)
    qkv_rows = qkv_rows.reshape(3, -1, group_qkv)
    qkv_full = jnp.moveaxis(in_order(spread_out(qkv_rows, "a"), "a"), 0, 1)
    qkv_full = qkv_full.reshape(3, width, group_qkv)

    vectors = gather_features(jnp.concatenate([norm_gain, norm_bias], axis=0)).astype(wide)
    gains, biases = vectors[:5], vectors[5:]

    group_up = w_up.shape[1] // count_a
    up_parts = trade(
        lambda k: lax.dynamic_slice_in_dim(w_up, (own_a ^ k) * group_up, group_up, 1), "a"
    )
    up_full = lax.all_gather(in_order(up_parts, "a"), "b", axis=1, tiled=True)
    up_full = up_full.reshape(width, group_up)

    group_o = w_o.shape[0] // count_b
    o_parts = trade(
        lambda k: lax.dynamic_slice_in_dim(w_o, (own_b ^ k) * group_o, group_o, 0), "b"
    )
    o_cols = jnp.moveaxis(in_order(o_parts, "b"), 0, 1).reshape(group_o, -1)
    o_full = jnp.moveaxis(in_order(spread_out(o_cols, "a"), "a"), 0, 1)
    o_full = o_full.reshape(group_o, width)

    down_parts = trade(
        lambda k: lax.dynamic_slice_in_dim(w_down, (own_a ^ k) * group_up, group_up, 0), "a"
    )
    down_cols = in_order(down_parts, "a")
    down_full = lax.all_gather(down_cols[:, None], "b", axis=1, tiled=True)
    down_full = jnp.moveaxis(down_full, 2, 0).reshape(group_up, width)

    first_full = gather_features(mix_w1.T).T

    streams_half = []
    for stream_id in range(4):
        total = None
        for level in range(depth_hist):
            weight = mixin[:, stream_id * depth_hist + level][:, None]
            term = weight * hist[level].astype(wide)
            total = term if total is None else total + term
        streams_half.append(total)
    streams_half = jnp.stack(streams_half)
    streams = both(own_rows(streams_half, 1), swap(other_rows(streams_half, 1)), 2)

    normed_own = jnp.stack(
        [layer_norm(streams[s], gains[s][None], biases[s][None]).astype(low) for s in range(3)]
    )
    normed = gather_tokens(normed_own, "b")
    seg_pair = jnp.stack([own_rows(seg_ids.reshape(-1)), other_rows(seg_ids.reshape(-1))])
    segment = jnp.stack(spread_out(seg_pair, "b"), axis=1).reshape(-1, length)

    local_heads = group_qkv // HDIM

    def heads_of(values):
        return values.reshape(-1, length, local_heads, HDIM)

    cosine_table, sine_table = rotary_tables(length, ROT)
    positions = jnp.arange(length)
    causal = positions[:, None] >= positions[None, :]
    allowed = causal[None] & (segment[:, :, None] == segment[:, None, :])
    queries = rotate(heads_of(dot(normed[0], qkv_full[0])), cosine_table, sine_table).astype(low)
    keys_in = rotate(heads_of(dot(normed[1], qkv_full[1])), cosine_table, sine_table).astype(low)
    values_in = heads_of(dot(normed[2], qkv_full[2])).astype(low)
    scores = (
        jnp.einsum("nqhd,nkhd->nhqk", queries, keys_in, preferred_element_type=wide) * score_scale
    )
    scores = jnp.where(allowed[:, None], scores, -1e30)
    row_top = jnp.max(scores, axis=-1, keepdims=True)
    expo = jnp.exp(scores - row_top)
    probs = expo / jnp.sum(expo, axis=-1, keepdims=True)
    probs_low = probs.astype(low)
    context = jnp.einsum("nhqk,nkhd->nqhd", probs_low, values_in, preferred_element_type=wide)
    context = context.reshape(-1, local_heads * HDIM).astype(low)
    group_rows = context.shape[0] // count_c

    def part(values, which):
        return values[which * group_rows : (which + 1) * group_rows]

    attention = reduce_tokens(lambda which: dot(part(context, which), o_full), "b")
    resid = streams[3] + attention
    ffn_in = layer_norm(resid, gains[3][None], biases[3][None]).astype(low)
    ffn_all = gather_tokens(ffn_in, "a")
    up_rows = ffn_all.shape[0] // count_c

    def up_part(values, which):
        return values[which * up_rows : (which + 1) * up_rows]

    up_pre = dot(ffn_all, up_full)
    active = exact_gelu(up_pre).astype(low)
    ffn_out = reduce_tokens(lambda which: dot(up_part(active, which), down_full), "a")
    block_value = resid + ffn_out
    block_low = block_value.astype(low)
    block_out = both(block_low, swap(block_low), 0)
    mix_in = rms_scale(block_value, gains[4][None]).astype(low)
    mix_pre = dot(mix_in, first_full)
    mix_act = exact_gelu(mix_pre).astype(low)
    mix_value = dot(mix_act, mix_w2)
    mix_out = both(mix_value, swap(mix_value), 0)

    groups_count = loss_table.shape[0]
    group_picks = (
        own_rows(domain_ids)[:, None] == jnp.arange(groups_count, dtype=jnp.int32)[None, :]
    ).astype(wide)
    token_weight = jnp.sum(group_picks * loss_table[None, :], axis=1, keepdims=True)
    mix_grad = own_rows(mix_cot) * token_weight
    block_grad = own_rows(out_cot).astype(wide) * token_weight
    act_grad = jnp.dot(mix_grad, mix_w2.astype(wide).T, precision=highest)
    w2_grad = jnp.dot(mix_act.astype(wide).T, mix_grad, precision=highest)
    pre_grad = jax.vjp(exact_gelu, mix_pre)[1](act_grad)[0]
    first_grad = jnp.dot(pre_grad.T, mix_in.astype(wide), precision=highest)
    norm_in_grad = jnp.dot(pre_grad, first_full.astype(wide).T, precision=highest)
    rms_block_grad, rms_gain_grad = jax.vjp(rms_scale, block_value, gains[4])[1](norm_in_grad)
    block_grad = block_grad + rms_block_grad
    w2_grad = add_over(add_over(add_over(w2_grad, "mp"), "b"), "a")

    block_all = gather_tokens(block_grad.astype(low), "a")
    up_pre_grad = jax.vjp(exact_gelu, up_pre)[1](across(block_all, down_full))[0].astype(low)
    ffn_in_grad = reduce_tokens(lambda which: across(up_part(up_pre_grad, which), up_full), "a")

    def hidden_grad(part_sum):
        summed = part_sum.astype(low).reshape(count_a, -1, group_up)
        summed = lax.psum_scatter(summed, "b", scatter_dimension=1, tiled=True)
        got = trade(
            lambda k: lax.dynamic_index_in_dim(summed, own_a ^ k, 0, keepdims=False), "a"
        )
        return jnp.moveaxis(in_order(got, "a"), 0, 1).reshape(-1, count_a * group_up)

    down_grad = hidden_grad(outer_sum(block_all, active)).T.astype(wide)
    up_grad = hidden_grad(outer_sum(ffn_all, up_pre_grad)).astype(wide)

    resid_from, ffn_gain_grad, ffn_bias_grad = jax.vjp(layer_norm, resid, gains[3], biases[3])[1](
        ffn_in_grad
    )
    resid_grad = block_grad + resid_from
    early = scatter_features(
        jnp.concatenate(
            [first_grad, rms_gain_grad[None], ffn_gain_grad[None], ffn_bias_grad[None]], axis=0
        )
    )
    resid_all = gather_tokens(resid_grad.astype(low), "b")
    context_grad = heads_of(across(resid_all, o_full).astype(low))
    prob_grad = jnp.einsum("nqhd,nkhd->nhqk", context_grad, values_in, preferred_element_type=wide)
    value_grad = jnp.einsum("nhqk,nqhd->nkhd", probs_low, context_grad, preferred_element_type=wide)
    score_grad = probs * (prob_grad - jnp.sum(probs * prob_grad, axis=-1, keepdims=True))
    score_grad = score_grad.astype(low)
    query_grad = (
        jnp.einsum("nhqk,nkhd->nqhd", score_grad, keys_in, preferred_element_type=wide)
        * score_scale
    )
    key_grad = (
        jnp.einsum("nhqk,nqhd->nkhd", score_grad, queries, preferred_element_type=wide)
        * score_scale
    )
    proj_lows = [
        value.reshape(-1, group_qkv).astype(low)
        for value in (
            rotate(query_grad, cosine_table, -sine_table),
            rotate(key_grad, cosine_table, -sine_table),
            value_grad,
        )
    ]
    normed_grad = reduce_tokens(
        lambda which: jnp.stack(
            [across(part(proj_lows[s], which), qkv_full[s]) for s in range(3)]
        ),
        "b",
    )

    def sum_over_a(blocks):
        got = trade(
            lambda k: lax.dynamic_index_in_dim(blocks, own_a ^ k, 0, keepdims=False).astype(
                low if k else wide
            ),
            "a",
        )
        total = got[0]
        for block in got[1:]:
            total = total + block.astype(wide)
        return total

    o_sum = sum_over_a(outer_sum(resid_all, context).reshape(count_a, -1, group_o)).astype(low)
    o_sum = o_sum.reshape(count_b, -1, group_o)
    o_got = trade(lambda k: lax.dynamic_index_in_dim(o_sum, own_b ^ k, 0, keepdims=False), "b")
    out_proj_grad = jnp.moveaxis(in_order(o_got, "b"), 1, 2).reshape(count_b * group_o, -1)

    qkv_sum = jnp.stack(
        [
            sum_over_a(outer_sum(normed[s], proj_lows[s]).reshape(count_a, -1, group_qkv))
            for s in range(3)
        ]
    )
    qkv_sum = qkv_sum.astype(low).reshape(3, count_b, -1, group_qkv)
    qkv_got = trade(lambda k: lax.dynamic_index_in_dim(qkv_sum, own_b ^ k, 1, keepdims=False), "b")
    proj_grads = jnp.moveaxis(in_order(qkv_got, "b"), 0, 2).reshape(3, -1, count_b * group_qkv)

    stream_grads, gain_rows, bias_rows = [], [], []
    for s in range(3):
        part_grad, part_gain, part_bias = jax.vjp(layer_norm, streams[s], gains[s], biases[s])[1](
            normed_grad[s]
        )
        stream_grads.append(part_grad)
        gain_rows.append(part_gain)
        bias_rows.append(part_bias)
    stream_grads.append(resid_grad)
    late = scatter_features(jnp.stack(gain_rows + bias_rows))

    stream_grad = jnp.stack(stream_grads)
    mine = lax.dynamic_slice_in_dim(stream_grad, own_c * half_width, half_width, 2)
    theirs = lax.dynamic_slice_in_dim(stream_grad, (1 - own_c) * half_width, half_width, 2)
    stream_half = both(mine, swap(theirs.astype(low)).astype(wide), 1)
    hist_grads = []
    mixin_cols = [[] for _ in range(4)]
    for level in range(depth_hist):
        total = None
        level_wide = hist[level].astype(wide)
        for s in range(4):
            term = mixin[:, s * depth_hist + level][:, None] * stream_half[s]
            total = term if total is None else total + term
            mixin_cols[s].append(jnp.sum(stream_half[s] * level_wide, axis=1))
        hist_grads.append(total)
    mixin_grad = jnp.stack([col for cols in mixin_cols for col in cols], axis=1)
    mixin_grad = mixin_grad + swap(mixin_grad)

    hidden_mix = mix_w1.shape[1]
    gain_grad = jnp.concatenate(
        [late[:3], early[hidden_mix + 1 : hidden_mix + 2], early[hidden_mix : hidden_mix + 1]]
    )
    bias_grad = jnp.concatenate([late[3:], early[hidden_mix + 2 :]])
    return (
        block_out,
        mix_out,
        jnp.stack(hist_grads),
        mixin_grad,
        proj_grads.astype(wide),
        out_proj_grad.astype(wide),
        up_grad,
        down_grad,
        early[:hidden_mix].T,
        w2_grad,
        gain_grad,
        bias_grad,
    )


def solution(mesh):
    spots = mesh.shape["dp"]
    grid = Mesh(
        mesh.devices.reshape(spots // INNER, INNER, mesh.shape["mp"]), ("a", "b", "mp")
    )
    dp = ("a", "b")
    in_specs = (
        P(None, dp, "mp"),
        P(dp, None),
        P(dp, None),
        P(dp),
        P(),
        P(None, dp, "mp"),
        P("mp", dp),
        P(dp, "mp"),
        P("mp", dp),
        P(dp, None),
        P(),
        P(None, dp),
        P(None, dp),
        P(dp, None),
        P(dp, None),
    )
    out_specs = (
        P(dp, None),
        P(dp, None),
        P(None, dp, "mp"),
        P(dp, None),
        P(None, dp, "mp"),
        P("mp", dp),
        P(dp, "mp"),
        P("mp", dp),
        P(dp, None),
        P(),
        P(None, dp),
        P(None, dp),
    )
    return jax.shard_map(body, mesh=grid, in_specs=in_specs, out_specs=out_specs, check_vma=False)
```

```python
import jax
import jax.numpy as jnp
from jax import lax
from jax.experimental import pallas as pl
from jax.experimental.pallas import tpu as pltpu
from jax.sharding import Mesh
from jax.sharding import PartitionSpec as P

HDIM = 128
ROT = 32
INNER = 4


highest = lax.Precision.HIGHEST
eps_norm = 1e-05
eps_rms = 1e-06
low = jnp.bfloat16
wide = jnp.float32


def layer_norm(values, gain_row, bias_row):
    center = values - jnp.mean(values, axis=-1, keepdims=True)
    spread = jnp.mean(center * center, axis=-1, keepdims=True)
    return center * lax.rsqrt(spread + eps_norm) * gain_row + bias_row


def rms_scale(values, gain_row):
    return (
        values * lax.rsqrt(jnp.mean(values * values, axis=-1, keepdims=True) + eps_rms) * gain_row
    )


def exact_gelu(values):
    return jax.nn.gelu(values, approximate=False)


def rotary_tables(length, rotated):
    half_rot = rotated // 2
    frequency = 10000.0 ** (-2.0 * jnp.arange(half_rot, dtype=wide) / rotated)
    angles = jnp.arange(length, dtype=wide)[:, None] * frequency[None, :]
    return (jnp.cos(angles), jnp.sin(angles))


def rotate(values, cosine_table, sine_table):
    half_rot = ROT // 2
    first_part = values[..., :half_rot]
    second = values[..., half_rot:ROT]
    cosine_b = cosine_table[:, None, :]
    sine_b = sine_table[:, None, :]
    return jnp.concatenate(
        [
            first_part * cosine_b - second * sine_b,
            second * cosine_b + first_part * sine_b,
            values[..., ROT:],
        ],
        axis=-1,
    )


def dot(left, right):
    return jnp.dot(left, right, preferred_element_type=wide)


def outer_sum(left_rows, right_rows):
    return lax.dot_general(
        left_rows, right_rows, (((0,), (0,)), ((), ())), preferred_element_type=wide
    )


def across(grad_rows, weight):
    return lax.dot_general(
        grad_rows, weight, (((1,), (1,)), ((), ())), preferred_element_type=wide
    )


def swap(values):
    return lax.ppermute(values, "mp", [(0, 1), (1, 0)])


def hop(values, axis, distance):
    count = lax.axis_size(axis)
    return lax.ppermute(values, axis, [(spot, spot ^ distance) for spot in range(count)])


def spread_out(values, axis):
    return [values] + [hop(values, axis, k) for k in range(1, lax.axis_size(axis))]


def trade(pick, axis):
    return [pick(0)] + [hop(pick(k), axis, k) for k in range(1, lax.axis_size(axis))]


def in_order(blocks, axis):
    own = lax.axis_index(axis)
    stacked = jnp.zeros((len(blocks),) + blocks[0].shape, blocks[0].dtype)
    for k, block in enumerate(blocks):
        stacked = lax.dynamic_update_index_in_dim(stacked, block, own ^ k, 0)
    return stacked


def gather_tokens(rows, axis):
    own = jnp.concatenate(spread_out(rows, axis), axis=-2)
    return jnp.concatenate([own, swap(own)], axis=-2)


def reduce_tokens(partial_of, axis):
    count = lax.axis_size(axis)
    theirs = partial_of(1).astype(low)
    mine = partial_of(0)
    mine = mine + swap(theirs).astype(wide)
    blocks = jnp.split(mine, count, axis=-2)
    got = trade(lambda k: blocks[k] if k == 0 else blocks[k].astype(low), axis)
    total = got[0]
    for block in got[1:]:
        total = total + block.astype(wide)
    return total


def add_over(values, axis):
    distance = 1
    while distance < lax.axis_size(axis):
        values = values + hop(values, axis, distance)
        distance *= 2
    return values


def scatter_features(rows):
    count_a, count_b = lax.axis_size("a"), lax.axis_size("b")
    own_a, own_b = lax.axis_index("a"), lax.axis_index("b")
    height = rows.shape[0]
    rows = rows + swap(rows)
    by_a = rows.reshape(height, count_a, -1)
    got = trade(lambda k: lax.dynamic_index_in_dim(by_a, own_a ^ k, 1, keepdims=False), "a")
    rows = sum(got[1:], got[0])
    by_b = rows.reshape(height, count_b, -1)
    got = trade(lambda k: lax.dynamic_index_in_dim(by_b, own_b ^ k, 1, keepdims=False), "b")
    return sum(got[1:], got[0])


def gather_features(rows):
    height = rows.shape[0]
    rows = in_order(spread_out(rows, "b"), "b")
    rows = in_order(spread_out(rows, "a"), "a")
    return jnp.moveaxis(rows, 2, 0).reshape(height, -1)


def body(
    hist,
    mixin,
    seg_ids,
    domain_ids,
    loss_table,
    w_qkv,
    w_o,
    w_up,
    w_down,
    mix_w1,
    mix_w2,
    norm_gain,
    norm_bias,
    out_cot,
    mix_cot,
):
    count_a, count_b, count_c = lax.axis_size("a"), lax.axis_size("b"), lax.axis_size("mp")
    own_a, own_b, own_c = lax.axis_index("a"), lax.axis_index("b"), lax.axis_index("mp")
    depth_hist, chip_tokens, half_width = hist.shape
    length = seg_ids.shape[1]
    width = half_width * count_c
    score_scale = HDIM ** (-0.5)
    rows_here = chip_tokens // count_c
    first = own_c == 0

    def own_rows(values, axis=0):
        return lax.dynamic_slice_in_dim(values, own_c * rows_here, rows_here, axis)

    def other_rows(values, axis=0):
        return lax.dynamic_slice_in_dim(values, (1 - own_c) * rows_here, rows_here, axis)

    def both(mine, theirs, axis):
        return jnp.concatenate(
            [jnp.where(first, mine, theirs), jnp.where(first, theirs, mine)], axis=axis
        )

    group_qkv = w_qkv.shape[2] // count_b
    qkv_parts = trade(
        lambda k: lax.dynamic_slice_in_dim(w_qkv, (own_b ^ k) * group_qkv, group_qkv, 2), "b"
    )
    qkv_rows = jnp.moveaxis(in_order(qkv_parts, "b"), 0, 1)
    qkv_rows = qkv_rows.reshape(3, -1, group_qkv)
    qkv_full = jnp.moveaxis(in_order(spread_out(qkv_rows, "a"), "a"), 0, 1)
    qkv_full = qkv_full.reshape(3, width, group_qkv)

    vectors = gather_features(jnp.concatenate([norm_gain, norm_bias], axis=0)).astype(wide)
    gains, biases = vectors[:5], vectors[5:]

    group_up = w_up.shape[1] // count_a
    up_parts = trade(
        lambda k: lax.dynamic_slice_in_dim(w_up, (own_a ^ k) * group_up, group_up, 1), "a"
    )
    up_full = lax.all_gather(in_order(up_parts, "a"), "b", axis=1, tiled=True)
    up_full = up_full.reshape(width, group_up)

    group_o = w_o.shape[0] // count_b
    o_parts = trade(
        lambda k: lax.dynamic_slice_in_dim(w_o, (own_b ^ k) * group_o, group_o, 0), "b"
    )
    o_cols = jnp.moveaxis(in_order(o_parts, "b"), 0, 1).reshape(group_o, -1)
    o_full = jnp.moveaxis(in_order(spread_out(o_cols, "a"), "a"), 0, 1)
    o_full = o_full.reshape(group_o, width)

    down_parts = trade(
        lambda k: lax.dynamic_slice_in_dim(w_down, (own_a ^ k) * group_up, group_up, 0), "a"
    )
    down_cols = in_order(down_parts, "a")
    down_full = lax.all_gather(down_cols[:, None], "b", axis=1, tiled=True)
    down_full = jnp.moveaxis(down_full, 2, 0).reshape(group_up, width)

    first_full = gather_features(mix_w1.T).T

    streams_half = []
    for stream_id in range(4):
        total = None
        for level in range(depth_hist):
            weight = mixin[:, stream_id * depth_hist + level][:, None]
            term = weight * hist[level].astype(wide)
            total = term if total is None else total + term
        streams_half.append(total)
    streams_half = jnp.stack(streams_half)
    streams = both(own_rows(streams_half, 1), swap(other_rows(streams_half, 1)), 2)

    normed_own = jnp.stack(
        [layer_norm(streams[s], gains[s][None], biases[s][None]).astype(low) for s in range(3)]
    )
    normed = gather_tokens(normed_own, "b")
    seg_pair = jnp.stack([own_rows(seg_ids.reshape(-1)), other_rows(seg_ids.reshape(-1))])
    segment = jnp.stack(spread_out(seg_pair, "b"), axis=1).reshape(-1, length)

    local_heads = group_qkv // HDIM

    def heads_of(values):
        return values.reshape(-1, length, local_heads, HDIM)

    cosine_table, sine_table = rotary_tables(length, ROT)
    positions = jnp.arange(length)
    causal = positions[:, None] >= positions[None, :]
    allowed = causal[None] & (segment[:, :, None] == segment[:, None, :])
    queries = rotate(heads_of(dot(normed[0], qkv_full[0])), cosine_table, sine_table).astype(low)
    keys_in = rotate(heads_of(dot(normed[1], qkv_full[1])), cosine_table, sine_table).astype(low)
    values_in = heads_of(dot(normed[2], qkv_full[2])).astype(low)
    scores = (
        jnp.einsum("nqhd,nkhd->nhqk", queries, keys_in, preferred_element_type=wide) * score_scale
    )
    scores = jnp.where(allowed[:, None], scores, -1e30)
    row_top = jnp.max(scores, axis=-1, keepdims=True)
    expo = jnp.exp(scores - row_top)
    probs = expo / jnp.sum(expo, axis=-1, keepdims=True)
    probs_low = probs.astype(low)
    context = jnp.einsum("nhqk,nkhd->nqhd", probs_low, values_in, preferred_element_type=wide)
    context = context.reshape(-1, local_heads * HDIM).astype(low)
    group_rows = context.shape[0] // count_c

    def part(values, which):
        return values[which * group_rows : (which + 1) * group_rows]

    attention = reduce_tokens(lambda which: dot(part(context, which), o_full), "b")
    resid = streams[3] + attention
    ffn_in = layer_norm(resid, gains[3][None], biases[3][None]).astype(low)
    ffn_all = gather_tokens(ffn_in, "a")
    up_rows = ffn_all.shape[0] // count_c

    def up_part(values, which):
        return values[which * up_rows : (which + 1) * up_rows]

    up_pre = dot(ffn_all, up_full)
    active = exact_gelu(up_pre).astype(low)
    ffn_out = reduce_tokens(lambda which: dot(up_part(active, which), down_full), "a")
    block_value = resid + ffn_out
    block_low = block_value.astype(low)
    block_out = both(block_low, swap(block_low), 0)
    mix_in = rms_scale(block_value, gains[4][None]).astype(low)
    mix_pre = dot(mix_in, first_full)
    mix_act = exact_gelu(mix_pre).astype(low)
    mix_value = dot(mix_act, mix_w2)
    mix_out = both(mix_value, swap(mix_value), 0)

    groups_count = loss_table.shape[0]
    group_picks = (
        own_rows(domain_ids)[:, None] == jnp.arange(groups_count, dtype=jnp.int32)[None, :]
    ).astype(wide)
    token_weight = jnp.sum(group_picks * loss_table[None, :], axis=1, keepdims=True)
    mix_grad = own_rows(mix_cot) * token_weight
    block_grad = own_rows(out_cot).astype(wide) * token_weight
    act_grad = jnp.dot(mix_grad, mix_w2.astype(wide).T, precision=highest)
    w2_grad = jnp.dot(mix_act.astype(wide).T, mix_grad, precision=highest)
    pre_grad = jax.vjp(exact_gelu, mix_pre)[1](act_grad)[0]
    first_grad = jnp.dot(pre_grad.T, mix_in.astype(wide), precision=highest)
    norm_in_grad = jnp.dot(pre_grad, first_full.astype(wide).T, precision=highest)
    rms_block_grad, rms_gain_grad = jax.vjp(rms_scale, block_value, gains[4])[1](norm_in_grad)
    block_grad = block_grad + rms_block_grad
    w2_grad = add_over(add_over(add_over(w2_grad, "mp"), "b"), "a")

    block_all = gather_tokens(block_grad.astype(low), "a")
    up_pre_grad = jax.vjp(exact_gelu, up_pre)[1](across(block_all, down_full))[0].astype(low)
    ffn_in_grad = reduce_tokens(lambda which: across(up_part(up_pre_grad, which), up_full), "a")

    def hidden_grad(part_sum):
        summed = part_sum.astype(low).reshape(count_a, -1, group_up)
        summed = lax.psum_scatter(summed, "b", scatter_dimension=1, tiled=True)
        got = trade(
            lambda k: lax.dynamic_index_in_dim(summed, own_a ^ k, 0, keepdims=False), "a"
        )
        return jnp.moveaxis(in_order(got, "a"), 0, 1).reshape(-1, count_a * group_up)

    down_grad = hidden_grad(outer_sum(block_all, active)).T.astype(wide)
    up_grad = hidden_grad(outer_sum(ffn_all, up_pre_grad)).astype(wide)

    resid_from, ffn_gain_grad, ffn_bias_grad = jax.vjp(layer_norm, resid, gains[3], biases[3])[1](
        ffn_in_grad
    )
    resid_grad = block_grad + resid_from
    early = scatter_features(
        jnp.concatenate(
            [first_grad, rms_gain_grad[None], ffn_gain_grad[None], ffn_bias_grad[None]], axis=0
        )
    )
    resid_all = gather_tokens(resid_grad.astype(low), "b")
    context_grad = heads_of(across(resid_all, o_full).astype(low))
    prob_grad = jnp.einsum("nqhd,nkhd->nhqk", context_grad, values_in, preferred_element_type=wide)
    value_grad = jnp.einsum("nhqk,nqhd->nkhd", probs_low, context_grad, preferred_element_type=wide)
    score_grad = probs * (prob_grad - jnp.sum(probs * prob_grad, axis=-1, keepdims=True))
    score_grad = score_grad.astype(low)
    query_grad = (
        jnp.einsum("nhqk,nkhd->nqhd", score_grad, keys_in, preferred_element_type=wide)
        * score_scale
    )
    key_grad = (
        jnp.einsum("nhqk,nqhd->nkhd", score_grad, queries, preferred_element_type=wide)
        * score_scale
    )
    proj_lows = [
        value.reshape(-1, group_qkv).astype(low)
        for value in (
            rotate(query_grad, cosine_table, -sine_table),
            rotate(key_grad, cosine_table, -sine_table),
            value_grad,
        )
    ]
    normed_grad = reduce_tokens(
        lambda which: jnp.stack(
            [across(part(proj_lows[s], which), qkv_full[s]) for s in range(3)]
        ),
        "b",
    )

    def sum_over_a(blocks):
        got = trade(
            lambda k: lax.dynamic_index_in_dim(blocks, own_a ^ k, 0, keepdims=False).astype(
                low if k else wide
            ),
            "a",
        )
        total = got[0]
        for block in got[1:]:
            total = total + block.astype(wide)
        return total

    o_sum = sum_over_a(outer_sum(resid_all, context).reshape(count_a, -1, group_o)).astype(low)
    o_sum = o_sum.reshape(count_b, -1, group_o)
    o_got = trade(lambda k: lax.dynamic_index_in_dim(o_sum, own_b ^ k, 0, keepdims=False), "b")
    out_proj_grad = jnp.moveaxis(in_order(o_got, "b"), 1, 2).reshape(count_b * group_o, -1)

    qkv_sum = jnp.stack(
        [
            sum_over_a(outer_sum(normed[s], proj_lows[s]).reshape(count_a, -1, group_qkv))
            for s in range(3)
        ]
    )
    qkv_sum = qkv_sum.astype(low).reshape(3, count_b, -1, group_qkv)
    qkv_got = trade(lambda k: lax.dynamic_index_in_dim(qkv_sum, own_b ^ k, 1, keepdims=False), "b")
    proj_grads = jnp.moveaxis(in_order(qkv_got, "b"), 0, 2).reshape(3, -1, count_b * group_qkv)

    stream_grads, gain_rows, bias_rows = [], [], []
    for s in range(3):
        part_grad, part_gain, part_bias = jax.vjp(layer_norm, streams[s], gains[s], biases[s])[1](
            normed_grad[s]
        )
        stream_grads.append(part_grad)
        gain_rows.append(part_gain)
        bias_rows.append(part_bias)
    stream_grads.append(resid_grad)
    late = scatter_features(jnp.stack(gain_rows + bias_rows))

    stream_grad = jnp.stack(stream_grads)
    mine = lax.dynamic_slice_in_dim(stream_grad, own_c * half_width, half_width, 2)
    theirs = lax.dynamic_slice_in_dim(stream_grad, (1 - own_c) * half_width, half_width, 2)
    stream_half = both(mine, swap(theirs.astype(low)).astype(wide), 1)
    hist_grads = []
    mixin_cols = [[] for _ in range(4)]
    for level in range(depth_hist):
        total = None
        level_wide = hist[level].astype(wide)
        for s in range(4):
            term = mixin[:, s * depth_hist + level][:, None] * stream_half[s]
            total = term if total is None else total + term
            mixin_cols[s].append(jnp.sum(stream_half[s] * level_wide, axis=1))
        hist_grads.append(total)
    mixin_grad = jnp.stack([col for cols in mixin_cols for col in cols], axis=1)
    mixin_grad = mixin_grad + swap(mixin_grad)

    hidden_mix = mix_w1.shape[1]
    gain_grad = jnp.concatenate(
        [late[:3], early[hidden_mix + 1 : hidden_mix + 2], early[hidden_mix : hidden_mix + 1]]
    )
    bias_grad = jnp.concatenate([late[3:], early[hidden_mix + 2 :]])
    return (
        block_out,
        mix_out,
        jnp.stack(hist_grads),
        mixin_grad,
        proj_grads.astype(wide),
        out_proj_grad.astype(wide),
        up_grad,
        down_grad,
        early[:hidden_mix].T,
        w2_grad,
        gain_grad,
        bias_grad,
    )


whole = pl.BlockSpec(memory_space=pltpu.VMEM)
scalars = pl.BlockSpec(memory_space=pltpu.SMEM)
anywhere = pl.BlockSpec(memory_space=pl.ANY)


def shaped(shape, dtype=wide):
    return jax.ShapeDtypeStruct(tuple(shape), dtype)


def local_call(kernel, outs, spots, arrays, specs=None, scratch=(), flops=0):
    moved = sum(value.size * value.dtype.itemsize for value in list(arrays) + list(outs))
    return pl.pallas_call(
        kernel,
        out_shape=tuple(outs),
        in_specs=[scalars] + (specs or [whole] * len(arrays)),
        out_specs=tuple(whole for _ in outs),
        scratch_shapes=list(scratch),
        cost_estimate=pl.CostEstimate(flops=flops, bytes_accessed=moved, transcendentals=0),
    )(spots, *arrays)


def window(index, size):
    return pl.ds(pl.multiple_of(index * size, size), size)


def cut_weight(spots, weight, count, own_at, dim):
    size = weight.shape[dim] // count
    shape = list(weight.shape)
    shape[dim] = size

    def kernel(spots_ref, weight_ref, *refs):
        outs, sem = refs[:-1], refs[-1]
        copies = []
        for k in range(count):
            place = [slice(None)] * len(shape)
            place[dim] = window(spots_ref[own_at] ^ k, size)
            copies.append(pltpu.make_async_copy(weight_ref.at[tuple(place)], outs[k], sem.at[k]))
        for copy in copies:
            copy.start()
        for copy in copies:
            copy.wait()

    return local_call(
        kernel,
        [shaped(shape, weight.dtype)] * count,
        spots,
        [weight],
        specs=[anywhere],
        scratch=[pltpu.SemaphoreType.DMA((count,))],
    )


def place_blocks(spots, blocks, own_at, dim, dtype, transpose=False):
    shape = list(blocks[0].shape)
    if transpose:
        shape = shape[::-1]
    size = shape[dim]
    out = list(shape)
    out[dim] = size * len(blocks)

    def kernel(spots_ref, *refs):
        out_ref = refs[-1]
        for k, block in enumerate(refs[:-1]):
            place = [slice(None)] * len(out)
            place[dim] = window(spots_ref[own_at] ^ k, size)
            value = block[...].astype(dtype)
            out_ref[tuple(place)] = value.T if transpose else value

    return local_call(kernel, [shaped(out, dtype)], spots, blocks)[0]


def place_qkv_rows(spots, blocks, own_at):
    three, rows, cols = blocks[0].shape

    def kernel(spots_ref, *refs):
        out_ref = refs[-1]
        for k, block in enumerate(refs[:-1]):
            for s in range(three):
                out_ref[window(spots_ref[own_at] ^ k, rows), s * cols : (s + 1) * cols] = block[s]

    return local_call(
        kernel, [shaped((len(blocks) * rows, three * cols), blocks[0].dtype)], spots, blocks
    )[0]


def place_qkv_grad(spots, blocks, own_at):
    cols, rows = blocks[0].shape[0] // 3, blocks[0].shape[1]

    def kernel(spots_ref, *refs):
        out_ref = refs[-1]
        for k, block in enumerate(refs[:-1]):
            for s in range(3):
                part = block[s * cols : (s + 1) * cols].astype(wide)
                out_ref[s, :, window(spots_ref[own_at] ^ k, cols)] = part.T

    return local_call(kernel, [shaped((3, rows, len(blocks) * cols))], spots, blocks)[0]


def sum_and_cut(spots, parts, count, own_at, dim, sent, kept=wide):
    shape = list(parts[0].shape)
    size = shape[dim] // count
    shape[dim] = size

    def kernel(spots_ref, *refs):
        ins, outs = refs[: len(parts)], refs[len(parts) :]
        for k in range(count):
            place = [slice(None)] * len(shape)
            place[dim] = window(spots_ref[own_at] ^ k, size)
            total = ins[0][tuple(place)]
            if len(parts) > 1:
                total = total.astype(wide)
            for ref in ins[1:]:
                total = total + ref[tuple(place)].astype(wide)
            outs[k][...] = total.astype(outs[k].dtype)

    outs = [shaped(shape, kept if k == 0 else sent) for k in range(count)]
    return local_call(kernel, outs, spots, parts)


def stack_rows(spots, blocks):
    rows, cols = blocks[0].shape

    def kernel(spots_ref, *refs):
        for k, block in enumerate(refs[:-1]):
            refs[-1][k * rows : (k + 1) * rows] = block[...]

    return local_call(
        kernel, [shaped((rows * len(blocks), cols), blocks[0].dtype)], spots, blocks
    )[0]


def gather_blocks(rows, axis):
    mine = spread_out(rows, axis)
    return mine + [swap(block) for block in mine]


def mix_streams(spots, mixin, hist):
    depth, rows, cols = hist.shape
    step = 16
    half = rows // 2 // step
    group = mixin.shape[1]

    def kernel(spots_ref, mixin_ref, hist_ref, mine_ref, theirs_ref):
        def put(out_ref):
            levels = [hist_ref[j].astype(wide) for j in range(depth)]
            for s in range(4):
                total = None
                for j in range(depth):
                    at = s * depth + j
                    term = mixin_ref[:, at : at + 1] * levels[j]
                    total = term if total is None else total + term
                out_ref[s] = total

        @pl.when(pl.program_id(0) < half)
        def _():
            put(theirs_ref)

        @pl.when(pl.program_id(0) >= half)
        def _():
            put(mine_ref)

    def block(i, spots_ref):
        core = spots_ref[2]
        return jnp.where(i < half, (1 - core) * half + i, core * half + i - half)

    return pl.pallas_call(
        kernel,
        out_shape=(shaped((4, rows // 2, cols)), shaped((4, rows // 2, cols))),
        grid_spec=pltpu.PrefetchScalarGridSpec(
            num_scalar_prefetch=1,
            grid=(2 * half,),
            in_specs=[
                pl.BlockSpec((step, group), lambda i, r: (block(i, r), 0)),
                pl.BlockSpec((depth, step, cols), lambda i, r: (0, block(i, r), 0)),
            ],
            out_specs=(
                pl.BlockSpec((4, step, cols), lambda i, r: (0, jnp.maximum(i - half, 0), 0)),
                pl.BlockSpec((4, step, cols), lambda i, r: (0, jnp.minimum(i, half - 1), 0)),
            ),
        ),
        cost_estimate=pl.CostEstimate(
            flops=0, bytes_accessed=2 * hist.size + 16 * rows * cols, transcendentals=0
        ),
    )(spots, mixin, hist)


def mix_streams_back(spots, mixin, hist, mine, theirs):
    depth, rows, cols = hist.shape
    step = 16
    half = rows // 2 // step
    group = mixin.shape[1]

    def kernel(spots_ref, mixin_ref, hist_ref, mine_ref, theirs_ref, grad_ref, mixin_grad_ref):
        def put(in_ref):
            streams = [in_ref[s].astype(wide) for s in range(4)]
            lane = lax.broadcasted_iota(jnp.int32, (step, group), 1)
            sums = jnp.zeros((step, group), wide)
            for j in range(depth):
                level = hist_ref[j].astype(wide)
                total = None
                for s in range(4):
                    at = s * depth + j
                    term = mixin_ref[:, at : at + 1] * streams[s]
                    total = term if total is None else total + term
                    found = jnp.sum(streams[s] * level, axis=1, keepdims=True)
                    sums = jnp.where(lane == at, found, sums)
                grad_ref[j] = total
            mixin_grad_ref[...] = sums

        @pl.when(pl.program_id(0) < half)
        def _():
            put(mine_ref)

        @pl.when(pl.program_id(0) >= half)
        def _():
            put(theirs_ref)

    def block(i, spots_ref):
        core = spots_ref[2]
        return jnp.where(i < half, core * half + i, (1 - core) * half + i - half)

    return pl.pallas_call(
        kernel,
        out_shape=(shaped(hist.shape), shaped(mixin.shape)),
        grid_spec=pltpu.PrefetchScalarGridSpec(
            num_scalar_prefetch=1,
            grid=(2 * half,),
            in_specs=[
                pl.BlockSpec((step, group), lambda i, r: (block(i, r), 0)),
                pl.BlockSpec((depth, step, cols), lambda i, r: (0, block(i, r), 0)),
                pl.BlockSpec((4, step, cols), lambda i, r: (0, jnp.minimum(i, half - 1), 0)),
                pl.BlockSpec((4, step, cols), lambda i, r: (0, jnp.maximum(i - half, 0), 0)),
            ],
            out_specs=(
                pl.BlockSpec((depth, step, cols), lambda i, r: (0, block(i, r), 0)),
                pl.BlockSpec((step, group), lambda i, r: (block(i, r), 0)),
            ),
        ),
        cost_estimate=pl.CostEstimate(
            flops=0, bytes_accessed=6 * hist.size + 16 * rows * cols, transcendentals=0
        ),
    )(spots, mixin, hist, mine, theirs)


def normal_rows(values):
    center = values - jnp.mean(values, axis=-1, keepdims=True)
    spread = jnp.mean(center * center, axis=-1, keepdims=True)
    inverse = lax.rsqrt(spread + eps_norm)
    return center * inverse, inverse


def norm_back(normal, inverse, grad, gain):
    scaled = grad * gain
    return inverse * (
        scaled
        - jnp.mean(scaled, axis=-1, keepdims=True)
        - normal * jnp.mean(scaled * normal, axis=-1, keepdims=True)
    )


def norm_streams(spots, vectors, mine, theirs):
    rows, cols = mine.shape[1:]

    def kernel(spots_ref, vectors_ref, mine_ref, theirs_ref, streams_ref, normed_ref):
        core = spots_ref[2]
        for s in range(4):
            streams_ref[s, :, window(core, cols)] = mine_ref[s]
            streams_ref[s, :, window(1 - core, cols)] = theirs_ref[s]
        for s in range(3):
            gain = vectors_ref[s : s + 1].astype(wide)
            bias = vectors_ref[5 + s : 6 + s].astype(wide)
            normed_ref[s] = (normal_rows(streams_ref[s])[0] * gain + bias).astype(low)

    return local_call(
        kernel,
        [shaped((4, rows, 2 * cols)), shaped((3, rows, 2 * cols), low)],
        spots,
        [vectors, mine, theirs],
    )


def roll_lanes(values, shift):
    return pltpu.roll(values, shift % HDIM, axis=values.ndim - 1)


def turn(values, tables, sign):
    half_rot = ROT // 2
    moved = roll_lanes(values, -half_rot) * tables[1] + roll_lanes(values, half_rot) * tables[2]
    return values * tables[0] + (moved if sign > 0 else -moved)


def turn_tables(length):
    cosine, sine = rotary_tables(length, ROT)
    rest = HDIM - ROT
    nothing = jnp.zeros((length, ROT // 2), wide)
    return jnp.stack(
        [
            jnp.concatenate([cosine, cosine, jnp.ones((length, rest), wide)], axis=1),
            jnp.concatenate([-sine, nothing, jnp.zeros((length, rest), wide)], axis=1),
            jnp.concatenate([nothing, sine, jnp.zeros((length, rest), wide)], axis=1),
        ]
    )


def attend(spots, blocks, weight, segment, tables):
    length, width = blocks[0].shape[1:]
    count = len(blocks)
    cols = weight.shape[1] // 3
    heads = cols // HDIM
    rows = count * length
    scale = HDIM ** (-0.5)

    def kernel(spots_ref, *refs):
        ins = refs[:count]
        weight_ref, segment_ref, column_ref, tables_ref = refs[count : count + 4]
        normed_ref, proj_ref, probs_ref, context_ref = refs[count + 4 :]
        for t in range(count):
            normed_ref[:, t * length : (t + 1) * length] = ins[t][...]
        for s in range(3):
            found = jnp.dot(
                normed_ref[s],
                weight_ref[:, s * cols : (s + 1) * cols],
                preferred_element_type=wide,
            )
            for h in range(heads):
                one = found[:, h * HDIM : (h + 1) * HDIM]
                if s < 2:
                    one = turn(one.reshape(count, length, HDIM), tables_ref, 1)
                    one = one.reshape(rows, HDIM)
                at = s * cols + h * HDIM
                proj_ref[:, at : at + HDIM] = one.astype(low)
        earlier = lax.broadcasted_iota(jnp.int32, (length, length), 0) >= (
            lax.broadcasted_iota(jnp.int32, (length, length), 1)
        )
        for t in range(count):
            here = slice(t * length, (t + 1) * length)
            allowed = earlier & (column_ref[:, t : t + 1] == segment_ref[t : t + 1, :])
            for h in range(heads):
                query = proj_ref[here, h * HDIM : (h + 1) * HDIM]
                key = proj_ref[here, cols + h * HDIM : cols + (h + 1) * HDIM]
                value = proj_ref[here, 2 * cols + h * HDIM : 2 * cols + (h + 1) * HDIM]
                scores = across(query, key) * scale
                scores = jnp.where(allowed, scores, -1e30)
                expo = jnp.exp(scores - jnp.max(scores, axis=-1, keepdims=True))
                probs = expo / jnp.sum(expo, axis=-1, keepdims=True)
                probs_ref[t * heads + h] = probs
                context = jnp.dot(probs.astype(low), value, preferred_element_type=wide)
                context_ref[here, h * HDIM : (h + 1) * HDIM] = context.astype(low)

    return local_call(
        kernel,
        [
            shaped((3, rows, width), low),
            shaped((rows, 3 * cols), low),
            shaped((count * heads, length, length)),
            shaped((rows, cols), low),
        ],
        spots,
        list(blocks) + [weight, segment, segment.T, tables],
        flops=6 * rows * width * cols,
    )


def attend_back(spots, blocks, out_weight, proj, probs, tables):
    length, width = blocks[0].shape
    count = len(blocks)
    cols = proj.shape[1] // 3
    heads = cols // HDIM
    rows = count * length
    scale = HDIM ** (-0.5)

    def kernel(spots_ref, *refs):
        ins = refs[:count]
        weight_ref, proj_ref, probs_ref, tables_ref = refs[count : count + 4]
        grad_ref, out_ref = refs[count + 4 :]
        for t in range(count):
            grad_ref[t * length : (t + 1) * length] = ins[t][...]
        context_grad = across(grad_ref[...], weight_ref[...]).astype(low)
        turns = [tables_ref[i] for i in range(3)]
        for t in range(count):
            here = slice(t * length, (t + 1) * length)
            for h in range(heads):
                at = slice(h * HDIM, (h + 1) * HDIM)
                key_at = slice(cols + h * HDIM, cols + (h + 1) * HDIM)
                value_at = slice(2 * cols + h * HDIM, 2 * cols + (h + 1) * HDIM)
                grad = context_grad[here, at]
                prob = probs_ref[t * heads + h]
                prob_grad = across(grad, proj_ref[here, value_at])
                score_grad = prob * (
                    prob_grad - jnp.sum(prob * prob_grad, axis=-1, keepdims=True)
                )
                score_grad = score_grad.astype(low)
                query_grad = (
                    jnp.dot(score_grad, proj_ref[here, key_at], preferred_element_type=wide) * scale
                )
                key_grad = outer_sum(score_grad, proj_ref[here, at]) * scale
                out_ref[here, at] = turn(query_grad, turns, -1).astype(low)
                out_ref[here, key_at] = turn(key_grad, turns, -1).astype(low)
                out_ref[here, value_at] = outer_sum(prob.astype(low), grad).astype(low)

    return local_call(
        kernel,
        [shaped((rows, width), low), shaped((rows, 3 * cols), low)],
        spots,
        list(blocks) + [out_weight, proj, probs, tables],
        flops=2 * rows * width * cols,
    )


def regroup(count_a, count_b, to_natural):
    pairs = []
    for i in range(count_a):
        for j in range(count_b):
            natural, other = i * count_b + j, j * count_a + i
            pairs.append((natural, other) if to_natural else (other, natural))
    return pairs


def block_at(index, size):
    return slice(index * size, (index + 1) * size)


def after_attention(spots, vectors, streams, parts, counts):
    rows, width = streams.shape[1:]
    size = width // (counts[0] * counts[1])

    def kernel(spots_ref, vectors_ref, streams_ref, *refs):
        ins, (resid_ref, normed_ref) = refs[:-2], refs[-2:]
        total = streams_ref[3]
        for ref in ins:
            total = total + ref[...].astype(wide)
        resid_ref[...] = total
        normed = normal_rows(total)[0] * vectors_ref[3:4].astype(wide)
        normed = (normed + vectors_ref[8:9].astype(wide)).astype(low)
        for there, here in regroup(*counts, False):
            normed_ref[:, block_at(there, size)] = normed[:, block_at(here, size)]

    return local_call(
        kernel,
        [shaped((rows, width)), shaped((rows, width), low)],
        spots,
        [vectors, streams] + list(parts),
    )


def gelu_slope(values):
    tail = 0.5 * (1.0 + lax.erf(values * (0.5**0.5)))
    bell = jnp.exp(-0.5 * values * values) * ((2.0 * jnp.pi) ** -0.5)
    return tail, tail + values * bell


def turn_around(spots, vectors, resid, parts, mix_w2, out_cot, mix_cot, weight, counts):
    rows, width = resid.shape
    size = width // (counts[0] * counts[1])
    hidden, levels = mix_w2.shape

    def kernel(spots_ref, vectors_ref, resid_ref, w2_ref, out_cot_ref, cot_ref, weight_ref, *refs):
        ins, outs = refs[: len(parts)], refs[len(parts) :]
        block_ref, mix_ref, w2_grad_ref, early_ref, grad_ref, sent_ref = outs
        total = ins[0][...].astype(wide)
        for ref in ins[1:]:
            total = total + ref[...].astype(wide)
        for there, here in regroup(*counts, True):
            at = block_at(there, size)
            grad_ref[:, at] = resid_ref[:, at] + total[:, block_at(here, size)]
        value = grad_ref[...]
        block_ref[...] = value.astype(low)
        gain = vectors_ref[4:5].astype(wide)
        inverse = lax.rsqrt(jnp.mean(value * value, axis=-1, keepdims=True) + eps_rms)
        scaled = value * inverse
        mix_in = (scaled * gain).astype(low)
        first = vectors_ref[9:]
        pre = across(mix_in, first)
        share, slope = gelu_slope(pre)
        act = (pre * share).astype(low)
        mix_ref[...] = jnp.dot(act, w2_ref[...], preferred_element_type=wide)
        token = weight_ref[...]
        mix_grad = cot_ref[...] * token
        act_grad = lax.dot_general(
            mix_grad,
            w2_ref[...].astype(wide),
            (((1,), (1,)), ((), ())),
            precision=highest,
            preferred_element_type=wide,
        )
        w2_grad_ref[...] = lax.dot_general(
            act.astype(wide),
            mix_grad,
            (((0,), (0,)), ((), ())),
            precision=highest,
            preferred_element_type=wide,
        )
        pre_grad = act_grad * slope
        early_ref[:hidden] = lax.dot_general(
            pre_grad,
            mix_in.astype(wide),
            (((0,), (0,)), ((), ())),
            precision=highest,
            preferred_element_type=wide,
        )
        norm_grad = jnp.dot(
            pre_grad, first.astype(wide), precision=highest, preferred_element_type=wide
        )
        early_ref[hidden : hidden + 1] = jnp.sum(norm_grad * scaled, axis=0, keepdims=True)
        direct = norm_grad * gain
        back = inverse * (direct - scaled * jnp.mean(direct * scaled, axis=-1, keepdims=True))
        back = back + out_cot_ref[...].astype(wide) * token
        grad_ref[...] = back
        for there, here in regroup(*counts, False):
            sent_ref[:, block_at(there, size)] = back[:, block_at(here, size)].astype(low)

    return local_call(
        kernel,
        [
            shaped((rows, width), low),
            shaped((rows, levels)),
            shaped((hidden, levels)),
            shaped((hidden + 1, width)),
            shaped((rows, width)),
            shaped((rows, width), low),
        ],
        spots,
        [vectors, resid, mix_w2, out_cot, mix_cot, weight] + list(parts),
    )


def resid_back(spots, vectors, resid, block_grad, parts, counts):
    rows, width = resid.shape
    size = width // (counts[0] * counts[1])

    def kernel(spots_ref, vectors_ref, resid_ref, block_ref, *refs):
        ins, (grad_ref, sent_ref, rows_ref) = refs[: len(parts)], refs[len(parts) :]
        total = ins[0][...].astype(wide)
        for ref in ins[1:]:
            total = total + ref[...].astype(wide)
        for there, here in regroup(*counts, True):
            grad_ref[:, block_at(there, size)] = total[:, block_at(here, size)]
        grad = grad_ref[...]
        normal, inverse = normal_rows(resid_ref[...])
        rows_ref[0:1] = jnp.sum(grad * normal, axis=0, keepdims=True)
        rows_ref[1:2] = jnp.sum(grad, axis=0, keepdims=True)
        grad = block_ref[...] + norm_back(normal, inverse, grad, vectors_ref[3:4].astype(wide))
        grad_ref[...] = grad
        sent_ref[...] = grad.astype(low)

    return local_call(
        kernel,
        [shaped((rows, width)), shaped((rows, width), low), shaped((2, width))],
        spots,
        [vectors, resid, block_grad] + list(parts),
    )


def normed_back(spots, proj_grad, weight, which, count, received=None):
    rows = proj_grad.shape[0] // 2
    width, cols = weight.shape[0], weight.shape[1] // 3
    length = rows // count

    def kernel(spots_ref, grad_ref, weight_ref, *refs):
        for s in range(3):
            at = slice(s * cols, (s + 1) * cols)
            found = across(grad_ref[which * rows : (which + 1) * rows, at], weight_ref[:, at])
            if received is None:
                refs[0][s] = found.astype(low)
            else:
                found = found + refs[0][s].astype(wide)
                for k in range(count):
                    out_ref = refs[1 + k]
                    out_ref[s] = found[block_at(k, length)].astype(out_ref.dtype)

    if received is None:
        outs = [shaped((3, rows, width), low)]
    else:
        outs = [shaped((3, length, width), low if k else wide) for k in range(count)]
    arrays = [proj_grad, weight] + ([] if received is None else [received])
    return local_call(kernel, outs, spots, arrays, flops=6 * rows * width * cols)


def streams_back(spots, vectors, streams, resid_grad, parts):
    rows, width = resid_grad.shape
    half = width // 2

    def kernel(spots_ref, vectors_ref, streams_ref, resid_ref, *refs):
        ins, (mine_ref, theirs_ref, rows_ref) = refs[: len(parts)], refs[len(parts) :]
        first = spots_ref[2] == 0

        def put(s, value):
            left, right = value[:, :half], value[:, half:]
            mine_ref[s] = jnp.where(first, left, right)
            theirs_ref[s] = jnp.where(first, right, left).astype(low)

        for s in range(3):
            grad = ins[0][s]
            for ref in ins[1:]:
                grad = grad + ref[s].astype(wide)
            normal, inverse = normal_rows(streams_ref[s])
            rows_ref[s : s + 1] = jnp.sum(grad * normal, axis=0, keepdims=True)
            rows_ref[3 + s : 4 + s] = jnp.sum(grad, axis=0, keepdims=True)
            put(s, norm_back(normal, inverse, grad, vectors_ref[s : s + 1].astype(wide)))
        put(3, resid_ref[...])

    return local_call(
        kernel,
        [shaped((4, rows, half)), shaped((4, rows, half), low), shaped((6, width))],
        spots,
        [vectors, streams, resid_grad] + list(parts),
    )


def send_sums(theirs, mine, axis):
    mine = mine + swap(theirs).astype(wide)
    blocks = jnp.split(mine, lax.axis_size(axis), axis=-2)
    return trade(lambda k: blocks[k] if k == 0 else blocks[k].astype(low), axis)


def scatter_small(spots, rows, counts):
    parts = [rows, swap(rows)]
    cut = sum_and_cut(spots, parts, counts[0], 0, 1, wide)
    got = trade(lambda k: cut[k], "a")
    cut = sum_and_cut(spots, got, counts[1], 1, 1, wide)
    got = trade(lambda k: cut[k], "b")
    return sum(got[1:], got[0])


def lean_body(
    hist,
    mixin,
    seg_ids,
    domain_ids,
    loss_table,
    w_qkv,
    w_o,
    w_up,
    w_down,
    mix_w1,
    mix_w2,
    norm_gain,
    norm_bias,
    out_cot,
    mix_cot,
):
    counts = count_a, count_b = lax.axis_size("a"), lax.axis_size("b")
    count_c = lax.axis_size("mp")
    own_c = lax.axis_index("mp")
    spots = jnp.stack([lax.axis_index("a"), lax.axis_index("b"), own_c]).astype(jnp.int32)
    chip_tokens = hist.shape[1]
    length = seg_ids.shape[1]
    rows_here = chip_tokens // count_c
    first = own_c == 0

    def own_rows(values):
        return lax.dynamic_slice_in_dim(values, own_c * rows_here, rows_here, 0)

    def other_rows(values):
        return lax.dynamic_slice_in_dim(values, (1 - own_c) * rows_here, rows_here, 0)

    def both(mine, theirs):
        return jnp.concatenate([jnp.where(first, mine, theirs), jnp.where(first, theirs, mine)])

    cut = cut_weight(spots, w_qkv, count_b, 1, 2)
    got = trade(lambda k: cut[k], "b")
    qkv_full = lax.all_gather(place_qkv_rows(spots, got, 1), "a", axis=0, tiled=True)
    small = jnp.concatenate([norm_gain, norm_bias, mix_w1.T], axis=0)
    small = place_blocks(spots, spread_out(small, "b"), 1, 1, low)
    vectors = place_blocks(spots, spread_out(small, "a"), 0, 1, low)
    cut_up = cut_weight(spots, w_up, count_a, 0, 1)
    got = trade(lambda k: cut_up[k], "a")
    up_full = lax.all_gather(place_blocks(spots, got, 0, 0, low), "b", axis=0, tiled=True)
    cut_down = cut_weight(spots, w_down, count_a, 0, 0)
    got = trade(lambda k: cut_down[k], "a")
    down_full = lax.all_gather(place_blocks(spots, got, 0, 1, low), "b", axis=1, tiled=True)
    cut_o = cut_weight(spots, w_o, count_b, 1, 0)
    got = trade(lambda k: cut_o[k], "b")
    got = spread_out(place_blocks(spots, got, 1, 1, low), "a")
    o_full = place_blocks(spots, got, 0, 1, low)

    mine, theirs = mix_streams(spots, mixin, hist)
    streams, normed_own = norm_streams(spots, vectors, mine, swap(theirs))
    seg_pair = jnp.stack([own_rows(seg_ids.reshape(-1)), other_rows(seg_ids.reshape(-1))])
    segment = jnp.stack(spread_out(seg_pair, "b"), axis=1).reshape(-1, length)
    tables = turn_tables(length)
    normed, proj, probs, context = attend(
        spots, gather_blocks(normed_own, "b"), qkv_full, segment, tables
    )
    half = context.shape[0] // count_c
    parts = send_sums(dot(context[half:], o_full).astype(low), dot(context[:half], o_full), "b")
    resid, ffn_in = after_attention(spots, vectors, streams, parts, counts)
    ffn_all = stack_rows(spots, gather_blocks(ffn_in, "a"))
    half_up = ffn_all.shape[0] // count_c
    up_pre = dot(ffn_all, up_full)
    active = exact_gelu(up_pre).astype(low)
    parts = send_sums(
        dot(active[half_up:], down_full).astype(low), dot(active[:half_up], down_full), "a"
    )
    groups_count = loss_table.shape[0]
    group_picks = (
        own_rows(domain_ids)[:, None] == jnp.arange(groups_count, dtype=jnp.int32)[None, :]
    ).astype(wide)
    token_weight = jnp.sum(group_picks * loss_table[None, :], axis=1, keepdims=True)
    block_low, mix_value, w2_grad, early, block_grad, block_sent = turn_around(
        spots,
        vectors,
        resid,
        parts,
        mix_w2,
        own_rows(out_cot),
        own_rows(mix_cot),
        token_weight,
        counts,
    )
    block_out = both(block_low, swap(block_low))
    mix_out = both(mix_value, swap(mix_value))

    block_all = stack_rows(spots, gather_blocks(block_sent, "a"))
    up_pre_grad = jax.vjp(exact_gelu, up_pre)[1](across(block_all, down_full))[0].astype(low)
    parts = send_sums(
        across(up_pre_grad[half_up:], up_full).astype(low),
        across(up_pre_grad[:half_up], up_full),
        "a",
    )

    def hidden_parts(part_sum):
        summed = lax.psum_scatter(part_sum.astype(low), "b", scatter_dimension=0, tiled=True)
        cut = sum_and_cut(spots, [summed], count_a, 0, 0, low, low)
        return trade(lambda k: cut[k], "a")

    down_parts = hidden_parts(outer_sum(block_all, active))
    down_grad = place_blocks(spots, down_parts, 0, 0, wide, transpose=True)
    up_grad = place_blocks(spots, hidden_parts(outer_sum(ffn_all, up_pre_grad)), 0, 1, wide)
    resid_grad, resid_sent, resid_rows = resid_back(
        spots, vectors, resid, block_grad, parts, counts
    )
    resid_all, proj_grad = attend_back(
        spots, gather_blocks(resid_sent, "b"), o_full, proj, probs, tables
    )
    (theirs,) = normed_back(spots, proj_grad, qkv_full, 1, count_b)
    cut = normed_back(spots, proj_grad, qkv_full, 0, count_b, swap(theirs))
    parts = trade(lambda k: cut[k], "b")

    group = qkv_full.shape[1] // 3
    qkv_sum = jnp.concatenate(
        [
            outer_sum(proj_grad[:, s * group : (s + 1) * group], normed[s]).astype(low)
            for s in range(3)
        ]
    )
    cut = sum_and_cut(spots, [qkv_sum], count_a, 0, 1, low, low)
    got = trade(lambda k: cut[k], "a")
    cut = sum_and_cut(spots, got, count_b, 1, 1, low, low)
    proj_grads = place_qkv_grad(spots, trade(lambda k: cut[k], "b"), 1)

    cut = sum_and_cut(spots, [outer_sum(context, resid_all)], count_a, 0, 1, low)
    got = trade(lambda k: cut[k], "a")
    cut = sum_and_cut(spots, got, count_b, 1, 1, low, low)
    out_proj_grad = place_blocks(spots, trade(lambda k: cut[k], "b"), 1, 0, wide)

    mine, theirs, late = streams_back(spots, vectors, streams, resid_grad, parts)
    hist_grad, mixin_grad = mix_streams_back(spots, mixin, hist, mine, swap(theirs))
    mixin_grad = mixin_grad + swap(mixin_grad)
    late = scatter_small(spots, late, counts)
    early = scatter_small(spots, jnp.concatenate([early, resid_rows]), counts)
    w2_grad = add_over(add_over(add_over(w2_grad, "mp"), "b"), "a")

    hidden = mix_w1.shape[1]
    gain_grad = jnp.concatenate(
        [late[:3], early[hidden + 1 : hidden + 2], early[hidden : hidden + 1]]
    )
    bias_grad = jnp.concatenate([late[3:], early[hidden + 2 :]])
    return (
        block_out,
        mix_out,
        hist_grad,
        mixin_grad,
        proj_grads,
        out_proj_grad,
        up_grad,
        down_grad,
        early[:hidden].T,
        w2_grad,
        gain_grad,
        bias_grad,
    )


def solution(mesh):
    spots = mesh.shape["dp"]
    grid = Mesh(
        mesh.devices.reshape(spots // INNER, INNER, mesh.shape["mp"]), ("a", "b", "mp")
    )
    dp = ("a", "b")
    in_specs = (
        P(None, dp, "mp"),
        P(dp, None),
        P(dp, None),
        P(dp),
        P(),
        P(None, dp, "mp"),
        P("mp", dp),
        P(dp, "mp"),
        P("mp", dp),
        P(dp, None),
        P(),
        P(None, dp),
        P(None, dp),
        P(dp, None),
        P(dp, None),
    )
    out_specs = (
        P(dp, None),
        P(dp, None),
        P(None, dp, "mp"),
        P(dp, None),
        P(None, dp, "mp"),
        P("mp", dp),
        P(dp, "mp"),
        P("mp", dp),
        P(dp, None),
        P(),
        P(None, dp),
        P(None, dp),
    )

    def step(*arrays):
        even = arrays[1].shape[0] // spots == 2 * arrays[2].shape[1]
        lanes = arrays[6].shape[1] // spots % HDIM == 0
        chosen = lean_body if even and lanes else body
        return jax.shard_map(
            chosen, mesh=grid, in_specs=in_specs, out_specs=out_specs, check_vma=False
        )(*arrays)

    return step
```
